32 devices in a mesh: groups: 2 (over y), seq: 4 (over z), tp: 2 (over x), kv: 2 (over core).
Axes of the slice: x: 2, y: 2, z: 4, core: 2. Of those that a mesh axis runs over, the one named last changes fastest.
Arguments:
- events: bfloat16 [8, 512, 2048], P('groups', 'seq', ('tp', 'kv')), parts along dimension 0, may hold values from -6 to 6
- history_cache: bfloat16 [2, 8, 512, 1024], P(None, ('groups', 'seq'), None, ('tp', 'kv')), parts along dimension 1, may hold values from -6 to 6
- block_counts: int32 [8], P(('groups', 'seq')), parts along dimension 0, may hold values from 1 to 4
- semantic_ids: int32 [4, 128], P(None, ('groups', 'seq')), parts along dimension 1, may hold values from 0 to 4095
- beam_parents: int32 [3, 128], P(None, ('groups', 'seq')), parts along dimension 1, may hold values from 0 to 15
- query_weight: bfloat16 [2048, 2048], P('seq', ('tp', 'kv')), may hold values from -0.125 to 0.125
- keyval_weight: bfloat16 [2, 2048, 1024], P(None, 'seq', ('tp', 'kv')), may hold values from -0.125 to 0.125
- out_weight: bfloat16 [2048, 2048], P('seq', ('tp', 'kv')), may hold values from -0.125 to 0.125
- cross_weight: bfloat16 [2, 2048, 1024], P(None, 'seq', ('tp', 'kv')), may hold values from -0.125 to 0.125
- decoder_query: bfloat16 [2048, 2048], P(None, ('tp', 'kv')), may hold values from -0.125 to 0.125
- decoder_out: bfloat16 [2048, 2048], P(None, ('tp', 'kv')), may hold values from -0.125 to 0.125
- code_table: bfloat16 [4096, 2048], P(('tp', 'kv')), may hold values from -6 to 6
- encoder_gain: float32 [2048], replicated, may hold values from 0.25 to 1.75
- cross_gain: float32 [2048], replicated, may hold values from 0.25 to 1.75
- decoder_gain: float32 [2048], replicated, may hold values from 0.25 to 1.75
Outputs:
- encoded: bfloat16 [8, 512, 2048], P(('groups', 'seq'), ('tp', 'kv')), parts along dimension 0
- beam_state: bfloat16 [128, 2048], P(('groups', 'seq'), ('tp', 'kv')), parts along dimension 0
The draws below stay inside these ranges and needn't reach their ends.
There are 2 independent parts, one for each index of `groups`. The reference program is written for one: setup_inputs(seed, part) draws one part's arguments, and reference() takes and returns one part's arrays. A program takes and returns all parts, laid end to end along the dimension named above; an argument that names none is the same for every part. Nothing has to cross between parts.
Inputs may be any that keep to these rules, and one draw needn't show every extreme that they name: A user's first 128 * block_counts new events are real; the rest are padding. `semantic_ids`: the codebook entry decoded for each beam row. `beam_parents`: the beam of the previous step that each beam row continues, counted among its user's 16 beams.
All inputs are finite; a program needn't handle non-finite values.
Results may differ from the reference program's by a relative error of at most 0.014.
Values may be sent and summed in bfloat16 or wider, within the bound.
A program may use at most 64 MiB of HBM per device.

```python
import jax
import jax.numpy as jnp
from jax import lax

D = 2048
H = 16
DH = 128
KVH = 8
V = 4096
EV = 512
BLK = 128
HIST = 512
BEAMS = 16
STEPS = 4
USERS = 4
N_TP = 2
N_KV = 2


def touch_ends(array, stream_key, low, largest):
    longest = array.shape.index(max(array.shape))
    spots = []
    for shift in (0, 1):
        where = [jax.random.randint(jax.random.fold_in(stream_key, axis), (), 0, length) for axis, length in enumerate(array.shape)]
        where[longest] = (where[longest] + shift) % array.shape[longest]
        spots.append(tuple(where))
    return array.at[spots[0]].set(low).at[spots[1]].set(largest)


def levels(rng, dims, cuts, smallest, top_value):
    gain, own = 1.0, jax.random.fold_in(rng, 6)
    for dim, blocks in cuts:
        heights = jnp.exp(jax.random.uniform(jax.random.fold_in(own, dim), (blocks,), jnp.float32, smallest / len(cuts), top_value / len(cuts)))
        gain = gain * jnp.repeat(heights, dims[dim] // blocks).reshape([-1 if axis == dim else 1 for axis in range(len(dims))])
    return gain


def scatter_about(rng, dims, scale, limit, split=(), held_as=jnp.bfloat16):
    values = jax.random.normal(rng, dims, jnp.float32) * scale
    if len(split) > 0:
        values = levels(rng, dims, split, -0.22, 0.18) * values
    return jnp.clip(values, min=-limit, max=limit).astype(held_as)


def setup_inputs(seed: int = 0, part: int = 0) -> dict:
    keys = jax.random.split(jax.random.key(seed), 16)
    part_keys = jax.random.split(jax.random.fold_in(keys[15], part), 16)
    return {
        "events": scatter_about(part_keys[0], (USERS, EV, D), 1.0, 6.0, ((1, 4), (2, 4))),
        "history_cache": scatter_about(part_keys[1], (2, USERS, HIST, KVH * DH), 1.0, 6.0, ((1, 4), (3, 4))),
        "block_counts": touch_ends(jax.random.randint(part_keys[2], (USERS,), 1, EV // BLK + 1), jax.random.fold_in(part_keys[2], 1), 1, (EV // BLK + 1) - 1).astype(jnp.int32),
        "semantic_ids": touch_ends(jax.random.randint(part_keys[3], (STEPS, USERS * BEAMS), 0, V), jax.random.fold_in(part_keys[3], 1), 0, V - 1).astype(jnp.int32),
        "beam_parents": touch_ends(jax.random.randint(part_keys[4], (STEPS - 1, USERS * BEAMS), 0, BEAMS), jax.random.fold_in(part_keys[4], 1), 0, BEAMS - 1).astype(jnp.int32),
        "query_weight": scatter_about(keys[5], (D, H * DH), D ** -0.5, 0.125, ((0, 4), (1, 4))),
        "keyval_weight": scatter_about(keys[6], (2, D, KVH * DH), D ** -0.5, 0.125, ((1, 4), (2, 4))),
        "out_weight": scatter_about(keys[7], (D, H * DH), (H * DH) ** -0.5, 0.125, ((0, 4), (1, 4))),
        "cross_weight": scatter_about(keys[8], (2, D, KVH * DH), D ** -0.5, 0.125, ((1, 4), (2, 4))),
        "decoder_query": scatter_about(keys[9], (D, H * DH), D ** -0.5, 0.125, ((1, 4),)),
        "decoder_out": scatter_about(keys[10], (D, H * DH), (H * DH) ** -0.5, 0.125, ((1, 4),)),
        "code_table": scatter_about(keys[11], (V, D), 1.0, 6.0, ((0, 4),)),
        "encoder_gain": jnp.clip(1.0 + 0.15 * jax.random.normal(keys[12], (D,), jnp.float32), 0.25, 1.75),
        "cross_gain": jnp.clip(1.0 + 0.15 * jax.random.normal(keys[13], (D,), jnp.float32), 0.25, 1.75),
        "decoder_gain": jnp.clip(1.0 + 0.15 * jax.random.normal(keys[14], (D,), jnp.float32), 0.25, 1.75),
    }


eps = 1e-06

def root_norm(values, scale_gain):
    mean_square = lax.optimization_barrier(jnp.mean(values * values, axis=-1, keepdims=True))
    return values * lax.rsqrt(mean_square + eps) * scale_gain.astype(jnp.float32)

def encode_user(item, query_weight, keyval_weight, out_weight, cross_weight, encoder_gain, cross_gain):
    user_events, user_cache, user_blocks = item
    groups = N_TP * N_KV
    per_group = H // groups
    group_ratio = H // KVH
    source = user_events.astype(jnp.float32)
    normed = root_norm(source, encoder_gain).astype(jnp.bfloat16)
    queries = jnp.dot(normed, query_weight, preferred_element_type=jnp.float32).astype(jnp.bfloat16)
    keys_new = jnp.dot(normed, keyval_weight[0], preferred_element_type=jnp.float32).astype(jnp.bfloat16)
    values_new = jnp.dot(normed, keyval_weight[1], preferred_element_type=jnp.float32).astype(jnp.bfloat16)
    keys_all = jnp.concatenate([user_cache[0], keys_new], axis=0)
    values_all = jnp.concatenate([user_cache[1], values_new], axis=0)
    query_heads = queries.reshape(EV, KVH, group_ratio, DH).astype(jnp.float32)
    key_heads = keys_all.reshape(HIST + EV, KVH, DH).astype(jnp.float32)
    value_heads = values_all.reshape(HIST + EV, KVH, DH).astype(jnp.float32)
    scores = jnp.einsum('igad,jgd->gaij', query_heads, key_heads) * DH ** (-0.5)
    query_index = jnp.arange(EV, dtype=jnp.int32)[:, None]
    key_index = jnp.arange(HIST + EV, dtype=jnp.int32)[None, :] - HIST
    visible = (key_index < 0) | (key_index <= query_index) & (key_index < user_blocks * BLK)
    raised = jnp.where(visible, jnp.exp(scores), jnp.float32(0.0))
    denominator = lax.optimization_barrier(jnp.sum(raised, axis=-1, keepdims=True))
    softened = (raised / denominator).astype(jnp.bfloat16)
    attended = jnp.einsum('gaij,jgd->igad', softened.astype(jnp.float32), value_heads)
    attended = attended.reshape(EV, H * DH).astype(jnp.bfloat16)
    grouped = attended.reshape(EV, groups, per_group * DH).astype(jnp.float32)
    out_grouped = out_weight.reshape(D, groups, per_group * DH).astype(jnp.float32)
    group_terms = jnp.einsum('igc,ogc->gio', grouped, out_grouped).astype(jnp.bfloat16)
    encoded_full = source + lax.optimization_barrier(jnp.sum(group_terms.astype(jnp.float32), axis=0))
    cross_in = root_norm(encoded_full, cross_gain).astype(jnp.bfloat16)
    cross_keys = jnp.dot(cross_in, cross_weight[0], preferred_element_type=jnp.float32).astype(jnp.bfloat16)
    cross_values = jnp.dot(cross_in, cross_weight[1], preferred_element_type=jnp.float32).astype(jnp.bfloat16)
    return (encoded_full.astype(jnp.bfloat16), cross_keys, cross_values)

def reference(events, history_cache, block_counts, semantic_ids, beam_parents, query_weight, keyval_weight, out_weight, cross_weight, decoder_query, decoder_out, code_table, encoder_gain, cross_gain, decoder_gain):
    cache_users = jnp.moveaxis(history_cache, 1, 0)
    encoded, cross_keys, cross_values = lax.map(lambda item: encode_user(item, query_weight, keyval_weight, out_weight, cross_weight, encoder_gain, cross_gain), (events, cache_users, block_counts))
    group_ratio = H // KVH
    key_heads = cross_keys.reshape(USERS, EV, KVH, DH).astype(jnp.float32)
    value_heads = cross_values.reshape(USERS, EV, KVH, DH).astype(jnp.float32)
    live_events = jnp.arange(EV, dtype=jnp.int32)[None, :] < (block_counts * BLK)[:, None]
    live_mask = live_events[:, None, None, None, :]

    def attend(beam_hidden):
        normed = root_norm(beam_hidden, decoder_gain).astype(jnp.bfloat16)
        beam_queries = jnp.dot(normed, decoder_query, preferred_element_type=jnp.float32).astype(jnp.bfloat16)
        query_heads = beam_queries.reshape(USERS, BEAMS, KVH, group_ratio, DH).astype(jnp.float32)
        beam_scores = jnp.einsum('ubgad,ujgd->ugabj', query_heads, key_heads) * DH ** (-0.5)
        raised = jnp.where(live_mask, jnp.exp(beam_scores), jnp.float32(0.0))
        denominator = lax.optimization_barrier(jnp.sum(raised, axis=-1, keepdims=True))
        softened = (raised / denominator).astype(jnp.bfloat16)
        attended = jnp.einsum('ugabj,ujgd->ubgad', softened.astype(jnp.float32), value_heads)
        attended = attended.reshape(USERS * BEAMS, H * DH).astype(jnp.bfloat16)
        return lax.dot_general(attended, decoder_out, (((1,), (1,)), ((), ())), preferred_element_type=jnp.float32)
    code_rows = code_table.astype(jnp.float32)
    all_rows = jnp.arange(USERS * BEAMS, dtype=jnp.int32)
    beam_hidden = jnp.take(code_rows, semantic_ids[0], axis=0)
    mixed_state = attend(beam_hidden)
    for level in range(1, STEPS):
        source_rows = all_rows // BEAMS * BEAMS + beam_parents[level - 1]
        beam_hidden = jnp.take(beam_hidden + mixed_state, source_rows, axis=0) + jnp.take(code_rows, semantic_ids[level], axis=0)
        mixed_state = attend(beam_hidden)
    return (encoded, (beam_hidden + mixed_state).astype(jnp.bfloat16))
```

```python
import functools

import jax
import jax.numpy as jnp
from jax import lax
from jax.experimental import pallas as pl
from jax.experimental.pallas import tpu as pltpu
from jax.sharding import PartitionSpec as P

DH = 128
BLK = 128
eps = 1e-06
F32 = jnp.float32
BF16 = jnp.bfloat16
MESH = pl.DeviceIdType.MESH


def unit_of(values):
    return lax.rsqrt(jnp.mean(values * values, axis=-1, keepdims=True) + eps)


def dot(a, b):
    return jnp.dot(a, b, preferred_element_type=F32)


def dot_t(a, b):
    return lax.dot_general(a, b, (((1,), (1,)), ((), ())), preferred_element_type=F32)


def subs_of(planes):
    return (4, 2, 2, 4, 2, 2) if planes <= 4 else (1,) * 6


def body(
    sizes,
    events, history, counts, ids, parents, wq_in, wkv_in, wo_in, wc_in, dq_in, do_in, table_in,
    egain, cgain, dgain,
    enc_out, beam_out,
    wq, wkv, wo, wc, dq, do, table, hist, xb, normed, res, qs, kn, vn, old, pold, pnew, att,
    gterm, rk, s1, rt, acc, cx, sc, ck, cv,
    look_own, look_in, look_sum, look_x, look, terms, last_own, last_in, hidden_ref, ba,
    local_sem, z_send, z_recv, y_send, y_recv, ev_send, ev_recv, xa_send, xa_recv,
    lk_send, lk_recv, rk_send, rk_recv, rt_send, rt_recv, cg_send, cg_recv, sc_send, sc_recv,
    tm_send, tm_recv,
):
    G, S, T, K = sizes
    TK = T * K
    g, s = lax.axis_index("groups"), lax.axis_index("seq")
    t, k = lax.axis_index("tp"), lax.axis_index("kv")
    p = t * K + k
    rows = wq_in.shape[0]
    part = rows // G
    width = wq.shape[0]
    length = normed.shape[0]
    block = length // S
    share = length // TK
    cols = wq.shape[1]
    kcols = kn.shape[1]
    beams = hidden_ref.shape[0]
    steps = ids.shape[0]
    chunks, _, feats = gterm.shape
    half = width // K

    def remote(src, dst, ss, rs, **where):
        return pltpu.make_async_remote_copy(
            src_ref=src, dst_ref=dst, send_sem=ss, recv_sem=rs, device_id=where, device_id_type=MESH
        )

    def wait_recv(ref, sem):
        remote(ref, ref, sem, sem, seq=s).wait_recv()

    def wait_send(ref, sem):
        remote(ref, ref, sem, sem, seq=s).wait_send()

    def inside(z):
        return jnp.logical_and(z >= 0, z < S)

    barrier = pltpu.get_barrier_semaphore()
    for j in range(1, S):
        pl.semaphore_signal(barrier, inc=1, device_id={"seq": lax.rem(s + j, S)}, device_id_type=MESH)
    for j in range(1, G):
        pl.semaphore_signal(barrier, inc=1, device_id={"groups": lax.rem(g + j, G)}, device_id_type=MESH)
    peers = []
    for j in range(1, TK):
        other = lax.rem(p + j, TK)
        peers.append((j - 1, other, lax.div(other, K), lax.rem(other, K)))
        pl.semaphore_signal(
            barrier, inc=1, device_id={"tp": peers[-1][2], "kv": peers[-1][3]}, device_id_type=MESH
        )

    mine = pl.ds(pl.multiple_of(s * rows, rows), rows)
    stay = pl.ds(pl.multiple_of(s * block, block), block)
    local = [
        pltpu.make_async_copy(a, b, local_sem.at[i])
        for i, (a, b) in enumerate(
            [
                (events.at[s], xb.at[p, stay]),
                (table_in, table),
                (wq_in, wq.at[mine]),
                (history.at[:, 0], hist),
                (wkv_in, wkv.at[:, mine]),
                (wo_in, wo.at[mine]),
                (wc_in, wc.at[:, mine]),
                (dq_in, dq),
                (do_in, do),
            ]
        )
    ]
    for copy in local:
        copy.start()
    pl.semaphore_wait(barrier, (S - 1) + (G - 1) + (TK - 1))

    for j in range(1, S):
        to = lax.rem(s + j, S)
        remote(events.at[to], xb.at[p, stay], ev_send.at[0], ev_recv.at[s], seq=to).start()

    weights = [
        (wq, wq_in, None), (wkv, wkv_in, 0), (wkv, wkv_in, 1),
        (wo, wo_in, None), (wc, wc_in, 0), (wc, wc_in, 1),
    ]
    Q, KEY, VALUE, OUT, CKEY, CVALUE = range(6)
    pieces = [(n, sub, of) for n, of in enumerate(subs_of(S)) for sub in range(of)]
    last = {n: i for i, (n, sub, of) in enumerate(pieces)}

    def view(ref, lead, start, size):
        where = pl.ds(pl.multiple_of(start, size), size)
        return ref.at[where] if lead is None else ref.at[lead, where]

    def at(i, origin):
        n, sub, of = pieces[i]
        size = part // of
        return view(weights[n][0], weights[n][2], origin * rows + g * part + sub * size, size)

    def own(i):
        n, sub, of = pieces[i]
        size = part // of
        return view(weights[n][1], weights[n][2], g * part + sub * size, size)

    up = (2 * s) // S
    ways = (2 * up - 1, 1 - 2 * up)

    def forward(i, way, r):
        step = ways[way]
        origin = s - step * r
        src = own(i) if r == 0 else at(i, origin)
        remote(src, at(i, origin), z_send.at[way, r], z_recv.at[i, origin], seq=s + step).start()

    def begin(i):
        for way in (0, 1):
            pl.when(inside(s + ways[way]))(functools.partial(forward, i, way, 0))

    def arrive(i, way, r):
        step = ways[way]
        origin = s - step * r

        def go():
            piece = at(i, origin)
            wait_recv(piece, z_recv.at[i, origin])
            if r + 1 < S:
                pl.when(inside(s + step))(functools.partial(forward, i, way, r))
            for j in range(1, G):
                remote(
                    piece, piece, y_send.at[way, r - 1, j - 1], y_recv.at[pieces[i][0], origin, j - 1],
                    groups=lax.rem(g + j, G),
                ).start()

        pl.when(inside(origin))(go)

    def settle(n, origin):
        def go():
            for j in range(1, G):
                half_of = view(
                    weights[n][0], weights[n][2], origin * rows + lax.rem(g - j + G, G) * part, part
                )
                wait_recv(half_of, y_recv.at[n, origin, j - 1])

        pl.when(origin != s)(go)

    def settle_all(n):
        for origin in range(S):
            settle(n, origin)

    progress = [0]
    AHEAD = 1
    LAG = 1

    def upto(goal):
        while progress[0] <= min(goal, len(pieces) - 1 + (S - 1) * LAG):
            now = progress[0]
            if now == 0:
                for i in range(min(AHEAD, len(pieces))):
                    begin(i)
            if now + AHEAD < len(pieces):
                begin(now + AHEAD)
            for way in (0, 1):
                for r in range(1, S):
                    if 0 <= now - r * LAG < len(pieces):
                        arrive(now - r * LAG, way, r)
            progress[0] += 1

    def arrived(n, r=None):
        upto(last[n] + LAG * (S - 1 if r is None else r))

    unit = part * sum(w[0].shape[-1] for w in weights) // cols

    def finish_weights():
        whole = wq.at[pl.ds(0, unit)]
        for way in (0, 1):
            step = ways[way]
            for r in range(S - 1):
                ok = jnp.logical_and(inside(s + step), inside(s - step * r))
                pl.when(ok)(functools.partial(wait_send, whole, z_send.at[way, r]))
            for r in range(1, S):
                for j in range(1, G):
                    pl.when(inside(s - step * r))(
                        functools.partial(wait_send, whole, y_send.at[way, r - 1, j - 1])
                    )

    def spread(piece_of, send_sem, recv_of):
        def give(source, **where):
            piece = piece_of(source)
            remote(piece, piece, send_sem, recv_of(source), **where).start()

        def take(source):
            wait_recv(piece_of(source), recv_of(source))

        def start():
            for i in range(1, T):
                give(p, tp=lax.rem(t + i, T))
            for j in range(1, K):
                give(p, kv=lax.rem(k + j, K))

        def relay():
            for i in range(1, T):
                there = lax.rem(t - i + T, T) * K + k
                take(there)
                for j in range(1, K):
                    give(there, kv=lax.rem(k + j, K))

        def finish():
            for j in range(1, K):
                for i in range(T):
                    take(lax.rem(t - i + T, T) * K + lax.rem(k - j + K, K))

        return start, relay, finish

    upto(0)

    def came(j):
        return pl.ds(pl.multiple_of(lax.rem(s - j + S, S) * block, block), block)

    moves = [
        spread(lambda q, j=j: xb.at[q, came(j)], xa_send.at[0], lambda q, j=j: xa_recv.at[j, q])
        for j in range(S)
    ]
    local[0].wait()
    moves[0][0]()

    local[1].wait()
    vocab = table.shape[0]
    column = jnp.zeros((steps * beams, 1), jnp.int32)
    line = lax.broadcasted_iota(jnp.int32, column.shape, 0)
    for r in range(steps * beams):
        column = jnp.where(line == r, ids[r // beams, r % beams], column)
    onehot = (
        column == p * vocab + lax.broadcasted_iota(jnp.int32, (steps * beams, vocab), 1)
    ).astype(BF16)
    for kk in range(K):
        for c in range(half // cols if half > cols else 1):
            wide = min(half, cols)
            look_own[kk, :, c * wide : (c + 1) * wide] = dot(
                onehot, table[:, kk * half + c * wide : kk * half + (c + 1) * wide]
            ).astype(BF16)
    for j in range(1, K):
        pk = lax.rem(k + j, K)
        remote(look_own.at[pk], look_in.at[j - 1], lk_send.at[0], lk_recv.at[0, j - 1], kv=pk).start()

    for j in range(1, S):
        wait_recv(xb.at[p, came(j)], ev_recv.at[lax.rem(s - j + S, S)])
        moves[j][0]()
    upto(1)
    moves[0][1]()

    for j in range(1, K):
        wait_recv(look_in.at[j - 1], lk_recv.at[0, j - 1])
    look_sum[...] = (
        look_own[k].astype(F32) + sum(look_in[j].astype(F32) for j in range(K - 1))
    ).astype(BF16)
    for i in range(1, T):
        remote(
            look_sum, look_x.at[i - 1], lk_send.at[1], lk_recv.at[1, i - 1], tp=lax.rem(t + i, T)
        ).start()

    for j in range(1, S):
        moves[j][1]()
    upto(2)
    for j in range(S):
        moves[j][2]()
        lines = came(j)
        source = [xb[q, lines].astype(F32) for q in range(TK)]
        square = sum(jnp.sum(v * v, axis=-1, keepdims=True) for v in source)
        scale = lax.rsqrt(square / width + eps)
        for q in range(TK):
            span = slice(q * cols, (q + 1) * cols)
            normed[lines, span] = (source[q] * scale * egain[:, span]).astype(BF16)
        if j == S // 2:
            upto(3)

    def lines_of(which):
        return pl.ds(pl.multiple_of(which * share, share), share)

    for q in range(TK):
        res[:, q * cols : (q + 1) * cols] = xb[q, lines_of(p)]
    for i in range(1, T):
        wait_recv(look_x.at[i - 1], lk_recv.at[1, i - 1])
    look[k] = (
        look_sum[...].astype(F32) + sum(look_x[i].astype(F32) for i in range(T - 1))
    ).astype(BF16)
    for j in range(1, K):
        remote(look.at[k], look.at[k], lk_send.at[2], lk_recv.at[2, j - 1], kv=lax.rem(k + j, K)).start()
    upto(4)
    for j in range(1, K):
        wait_recv(look.at[lax.rem(k - j + K, K)], lk_recv.at[2, j - 1])

    def code(level):
        lines = slice(level * beams, (level + 1) * beams)
        return jnp.concatenate([look[kk, lines] for kk in range(K)], axis=-1).astype(F32)

    def query(hidden):
        raw = dot((hidden * dgain[...]).astype(BF16), dq[...])
        return (raw * unit_of(hidden)).astype(BF16)

    local[7].wait()
    hidden_ref[...] = code(0)
    queries = query(hidden_ref[...])
    upto(5)

    local[2].wait()
    arrived(Q)
    settle_all(Q)
    qs[...] = dot(normed[...], wq[...]).astype(BF16)

    heads = cols // DH
    ratio = cols // kcols
    limit = counts[0] * BLK
    chunk = min(share, length)
    local[3].wait()
    for h in range(heads):
        hs = slice(h * DH, (h + 1) * DH)
        ks = slice(h // ratio * DH, (h // ratio + 1) * DH)
        for c in range(length // chunk):
            lines = slice(c * chunk, (c + 1) * chunk)
            old[h, lines] = jnp.exp(dot_t(qs[lines, hs], hist[0, :, ks]) * DH ** (-0.5))
        if h == heads // 2 - 1:
            upto(last[Q] + (S - 1) * LAG + 1)
    local[4].wait()
    arrived(KEY)
    settle_all(KEY)
    kn[...] = dot(normed[...], wkv[0]).astype(BF16)
    for h in range(heads):
        hs = slice(h * DH, (h + 1) * DH)
        ks = slice(h // ratio * DH, (h // ratio + 1) * DH)
        for c in range(length // chunk):
            lines = slice(c * chunk, (c + 1) * chunk)
            reach = (c + 1) * chunk
            new = jnp.exp(dot_t(qs[lines, hs], kn[:reach, ks]) * DH ** (-0.5))
            qi = lax.broadcasted_iota(jnp.int32, (chunk, reach), 0) + c * chunk
            ki = lax.broadcasted_iota(jnp.int32, (chunk, reach), 1)
            new = jnp.where((ki <= qi) & (ki < limit), new, 0.0)
            past = old[h, lines]
            total = jnp.sum(past, axis=-1, keepdims=True) + jnp.sum(new, axis=-1, keepdims=True)
            pold[h, lines] = (past / total).astype(BF16)
            pnew[h, lines, :reach] = (new / total).astype(BF16)
        if h == heads // 2 - 1:
            upto(last[KEY] + (S - 1) * LAG + 1)
    arrived(VALUE)
    settle_all(VALUE)
    vn[...] = dot(normed[...], wkv[1]).astype(BF16)
    for h in range(heads):
        hs = slice(h * DH, (h + 1) * DH)
        ks = slice(h // ratio * DH, (h // ratio + 1) * DH)
        for c in range(length // chunk):
            lines = slice(c * chunk, (c + 1) * chunk)
            reach = (c + 1) * chunk
            att[lines, hs] = (
                dot(pold[h, lines], hist[1, :, ks]) + dot(pnew[h, lines, :reach], vn[:reach, ks])
            ).astype(BF16)
    local[5].wait()

    in_turn = chunks == S and S & (S - 1) == 0

    def features(i):
        if not in_turn:
            return i
        at_plane, bit = 0, 1
        while bit < S:
            here = lax.rem(lax.div(s, bit), 2)
            at_plane = at_plane + bit * (1 - here if i & bit else here)
            bit *= 2
        return at_plane

    def span_of(i):
        return pl.ds(pl.multiple_of(features(i) * feats, feats), feats)

    def project(i):
        gterm[i] = dot_t(att[...], wo[span_of(i), :]).astype(BF16)
        for j in range(1, K):
            pk = lax.rem(k + j, K)
            for it in range(T):
                remote(
                    gterm.at[i, lines_of(lax.rem(t + 1 + it, T) * K + pk)], rk.at[i, j - 1, it],
                    rk_send.at[0], rk_recv.at[i, j - 1], kv=pk,
                ).start()

    def pass_on(i):
        for j in range(1, K):
            wait_recv(rk.at[i, j - 1], rk_recv.at[i, j - 1])
        for it in range(T):
            to = lax.rem(t + 1 + it, T)
            total = gterm[i, lines_of(to * K + k)].astype(F32)
            for j in range(1, K):
                total = total + rk[i, j - 1, it].astype(F32)
            if it < T - 1:
                s1[i, it] = total.astype(BF16)
                remote(s1.at[i, it], rt.at[i, it], rt_send.at[0], rt_recv.at[i, it], tp=to).start()
            else:
                acc[i] = total

    gathers = [
        spread(
            lambda q, i=i: cx.at[features(i), lines_of(q)], cg_send.at[0], lambda q, i=i: cg_recv.at[i, q]
        )
        for i in range(chunks)
    ]
    squares = []

    def complete(i):
        value = acc[i]
        for it in range(T - 1):
            wait_recv(rt.at[i, it], rt_recv.at[i, it])
            value = value + rt[i, it].astype(F32)
        value = value + res[:, span_of(i)].astype(F32)
        squares.append(jnp.sum(value * value, axis=-1, keepdims=True))
        cx[features(i), lines_of(p)] = (value * cgain[:, span_of(i)]).astype(BF16)
        gathers[i][0]()
        enc_out[:, span_of(i)] = value.astype(BF16)

    if not in_turn:
        arrived(OUT)
        settle_all(OUT)
    for i in range(chunks + 5):
        if i < chunks:
            if in_turn:
                arrived(OUT, i)
                if i > 0:
                    settle(OUT, features(i))
            project(i)
        else:
            upto(last[OUT] + (S - 1) * LAG + 1 + i - chunks)
        if 1 <= i < chunks + 1:
            pass_on(i - 1)
        if 2 <= i < chunks + 2:
            complete(i - 2)
            if i == chunks + 2 - 1:
                scale = lax.rsqrt(sum(squares) / width + eps)
                sc[p] = jnp.broadcast_to(scale, (share, 128))
                for slot, other, pt, pk in peers:
                    remote(sc.at[p], sc.at[p], sc_send.at[0], sc_recv.at[p], tp=pt, kv=pk).start()
        if 4 <= i < chunks + 4:
            gathers[i - 4][1]()
    arrived(CKEY)
    for slot, other, pt, pk in peers:
        wait_recv(sc.at[other], sc_recv.at[other])
    for start, relay, finish in gathers:
        finish()
    local[6].wait()
    settle_all(CKEY)
    by_row = sc[...].reshape(length, 128)[:, :1]

    def across(which):
        total = dot(cx[0], wc[which, :feats])
        for c in range(1, chunks):
            total = total + dot(cx[c], wc[which, c * feats : (c + 1) * feats])
        return (total * by_row).astype(BF16)

    ck[...] = across(0)
    live = lax.broadcasted_iota(jnp.int32, (ratio * beams, length), 1) < limit

    def soften(queries, j):
        ks = slice(j * DH, (j + 1) * DH)
        q = jnp.concatenate(
            [queries[:, (j * ratio + a) * DH : (j * ratio + a + 1) * DH] for a in range(ratio)], axis=0
        )
        raised = jnp.where(live, jnp.exp(dot_t(q, ck[:, ks]) * DH ** (-0.5)), 0.0)
        return (raised / jnp.sum(raised, axis=-1, keepdims=True)).astype(BF16)

    soft = [soften(queries, j) for j in range(kcols // DH)]
    local[8].wait()
    arrived(CVALUE)
    settle_all(CVALUE)
    cv[...] = across(1)

    for level in range(steps):
        if level > 0:
            soft = [soften(queries, j) for j in range(kcols // DH)]
        for j in range(kcols // DH):
            ks = slice(j * DH, (j + 1) * DH)
            found = dot(soft[j], cv[:, ks]).astype(BF16)
            for a in range(ratio):
                h = j * ratio + a
                ba[:, h * DH : (h + 1) * DH] = found[a * beams : (a + 1) * beams]
        if level < steps - 1:
            column = jnp.zeros((beams, 1), jnp.int32)
            line = lax.broadcasted_iota(jnp.int32, column.shape, 0)
            for r in range(beams):
                column = jnp.where(line == r, parents[level, r], column)
            pick = column == lax.broadcasted_iota(jnp.int32, (beams, beams), 1)
            picked = dot(pick.astype(BF16), ba[...]).astype(BF16)
            for c in range(TK):
                terms[level, p, c] = dot_t(picked, do[c * cols : (c + 1) * cols, :]).astype(BF16)
                for slot, other, pt, pk in peers:
                    piece = terms.at[level, p, c]
                    remote(piece, piece, tm_send.at[0], tm_recv.at[level, p], tp=pt, kv=pk).start()
            moved = jnp.dot(
                pick.astype(F32), hidden_ref[...], preferred_element_type=F32, precision=lax.Precision.HIGHEST
            )
            hidden_ref[...] = moved + code(level + 1)
            for slot, other, pt, pk in peers:
                wait_recv(terms.at[level, other], tm_recv.at[level, other])
            for c in range(TK):
                span = slice(c * cols, (c + 1) * cols)
                hidden_ref[:, span] = hidden_ref[:, span] + sum(
                    terms[level, q, c].astype(F32) for q in range(TK)
                )
            queries = query(hidden_ref[...])
        else:
            for c in range(TK):
                last_own[c] = dot_t(ba[...], do[c * cols : (c + 1) * cols, :]).astype(BF16)
            for slot, other, pt, pk in peers:
                remote(
                    last_own.at[other], last_in.at[slot], tm_send.at[1], tm_recv.at[level, slot], tp=pt, kv=pk
                ).start()
            value = jnp.zeros((beams, cols), F32)
            for c in range(TK):
                span = slice(c * cols, (c + 1) * cols)
                value = jnp.where(p == c, hidden_ref[:, span], value)
            value = value + last_own[p].astype(F32)
            for slot, other, pt, pk in peers:
                wait_recv(last_in.at[slot], tm_recv.at[level, slot])
            for slot in range(TK - 1):
                value = value + last_in[slot].astype(F32)
            beam_out[...] = value.astype(BF16)

    finish_weights()
    wait_send(xb.at[0, pl.ds(0, (S - 1) * block)], ev_send.at[0])
    wait_send(xb.at[pl.ds(0, TK - 1)], xa_send.at[0])
    wait_send(look_in, lk_send.at[0])
    wait_send(look_x, lk_send.at[1])
    wait_send(look_in, lk_send.at[2])
    wait_send(rk, rk_send.at[0])
    wait_send(rt, rt_send.at[0])
    wait_send(cx.at[:, pl.ds(0, (TK - 1) * share)], cg_send.at[0])
    wait_send(sc.at[pl.ds(0, TK - 1)], sc_send.at[0])
    wait_send(terms.at[pl.ds(0, steps - 1), pl.ds(0, TK - 1)], tm_send.at[0])
    wait_send(last_in, tm_send.at[1])


def solution(mesh):
    G, S, T, K = (mesh.shape[a] for a in ("groups", "seq", "tp", "kv"))
    TK = T * K

    def shards(
        events, history, counts, ids, parents, wq, wkv, wo, wc, dq, do, table, egain, cgain, dgain
    ):
        users, block, cols = events.shape
        length = block * S
        share = length // TK
        rows, kcols = wkv.shape[1:]
        width = rows * S
        steps, beams = ids.shape
        hist_len = history.shape[2]
        heads = cols // DH
        chunks = S if rows % 128 == 0 else TK
        feats = width // chunks
        pieces = sum(subs_of(S))
        vm = lambda *shape: pltpu.VMEM(shape, BF16)
        vf = lambda *shape: pltpu.VMEM(shape, F32)
        dma = lambda *shape: pltpu.SemaphoreType.DMA(shape)
        anywhere = pl.BlockSpec(memory_space=pl.ANY)
        vmem = pl.BlockSpec(memory_space=pltpu.VMEM)
        smem = pl.BlockSpec(memory_space=pltpu.SMEM)
        enc, beam = pl.pallas_call(
            functools.partial(body, (G, S, T, K)),
            out_shape=(
                jax.ShapeDtypeStruct((share, width), BF16),
                jax.ShapeDtypeStruct((beams, cols), BF16),
            ),
            in_specs=[anywhere, anywhere, smem, smem, smem] + [anywhere] * 7 + [vmem] * 3,
            out_specs=(vmem, vmem),
            scratch_shapes=[
                vm(width, cols), vm(2, width, kcols), vm(width, cols), vm(2, width, kcols),
                vm(width, cols), vm(width, cols), vm(*table.shape), vm(2, hist_len, kcols),
                vm(TK, length, cols), vm(length, width), vm(share, width),
                vm(length, cols), vm(length, kcols), vm(length, kcols),
                vf(heads, length, hist_len), vm(heads, length, hist_len), vm(heads, length, length),
                vm(length, cols),
                vm(chunks, length, feats), vm(chunks, K - 1, T, share, feats),
                vm(chunks, T - 1, share, feats), vm(chunks, T - 1, share, feats),
                vf(chunks, share, feats), vm(chunks, length, feats), vf(TK, share, 128),
                vm(length, kcols), vm(length, kcols),
                vm(K, steps * beams, width // K), vm(K - 1, steps * beams, width // K),
                vm(steps * beams, width // K), vm(T - 1, steps * beams, width // K),
                vm(K, steps * beams, width // K),
                vm(steps - 1, TK, TK, beams, cols), vm(TK, beams, cols), vm(TK - 1, beams, cols),
                vf(beams, width), vm(beams, cols),
                dma(9), dma(2, S - 1), dma(pieces, S), dma(2, S - 1, G - 1), dma(6, S, G - 1),
                dma(1), dma(S), dma(1), dma(S, TK),
                dma(3), dma(3, max(T, K) - 1), dma(1), dma(chunks, K - 1), dma(1), dma(chunks, T - 1),
                dma(1), dma(chunks, TK), dma(1), dma(TK),
                dma(2), dma(steps, TK),
            ],
            compiler_params=pltpu.CompilerParams(
                collective_id=0, has_side_effects=True, vmem_limit_bytes=60 * 1024 * 1024
            ),
        )(
            events, history, counts, ids, parents, wq, wkv, wo, wc, dq, do,
            table, egain[None], cgain[None], dgain[None],
        )
        return enc[None], beam

    in_specs = (
        P("groups", "seq", ("tp", "kv")),
        P(None, ("groups", "seq"), None, ("tp", "kv")),
        P(("groups", "seq")),
        P(None, ("groups", "seq")),
        P(None, ("groups", "seq")),
        P("seq", ("tp", "kv")),
        P(None, "seq", ("tp", "kv")),
        P("seq", ("tp", "kv")),
        P(None, "seq", ("tp", "kv")),
        P(None, ("tp", "kv")),
        P(None, ("tp", "kv")),
        P(("tp", "kv"), None),
        P(),
        P(),
        P(),
    )
    out_specs = (P(("groups", "seq"), ("tp", "kv"), None), P(("groups", "seq"), ("tp", "kv")))
    return jax.shard_map(shards, mesh=mesh, in_specs=in_specs, out_specs=out_specs, check_vma=False)
```

```python
import functools

import jax
import jax.numpy as jnp
from jax import lax
from jax.experimental import pallas as pl
from jax.experimental.pallas import tpu as pltpu
from jax.sharding import PartitionSpec as P

DH = 128
BLK = 128
eps = 1e-06
F32 = jnp.float32
BF16 = jnp.bfloat16
MESH = pl.DeviceIdType.MESH


def unit_of(values):
    return lax.rsqrt(jnp.mean(values * values, axis=-1, keepdims=True) + eps)


def dot(a, b):
    return jnp.dot(a, b, preferred_element_type=F32)


def dot_t(a, b):
    return lax.dot_general(a, b, (((1,), (1,)), ((), ())), preferred_element_type=F32)


def subs_of(planes):
    return (4, 2, 2, 4, 2, 2) if planes <= 4 else (1,) * 6


def body(
    sizes,
    events, history, counts, ids, parents, wq_in, wkv_in, wo_in, wc_in, dq_in, do_in, table_in,
    egain, cgain, dgain,
    enc_out, beam_out,
    wq, wkv, wo, wc, dq, do, table, hist, xb, normed, res, qs, kn, vn, old, pold, pnew, att,
    gterm, rk, s1, rt, acc, cx, sc, ck, cv,
    look_own, look_in, look_sum, look_x, look, terms, last_own, last_in, hidden_ref, ba,
    local_sem, z_send, z_recv, y_send, y_recv, ev_send, ev_recv, xa_send, xa_recv,
    lk_send, lk_recv, rk_send, rk_recv, rt_send, rt_recv, cg_send, cg_recv, sc_send, sc_recv,
    tm_send, tm_recv,
):
    G, S, T, K = sizes
    TK = T * K
    g, s = lax.axis_index("groups"), lax.axis_index("seq")
    t, k = lax.axis_index("tp"), lax.axis_index("kv")
    p = t * K + k
    rows = wq_in.shape[0]
    part = rows // G
    width = wq.shape[0]
    length = normed.shape[0]
    block = length // S
    share = length // TK
    cols = wq.shape[1]
    kcols = kn.shape[1]
    beams = hidden_ref.shape[0]
    steps = ids.shape[0]
    chunks, _, feats = gterm.shape
    half = width // K

    def remote(src, dst, ss, rs, **where):
        return pltpu.make_async_remote_copy(
            src_ref=src, dst_ref=dst, send_sem=ss, recv_sem=rs, device_id=where, device_id_type=MESH
        )

    def wait_recv(ref, sem):
        remote(ref, ref, sem, sem, seq=s).wait_recv()

    def wait_send(ref, sem):
        remote(ref, ref, sem, sem, seq=s).wait_send()

    def inside(z):
        return jnp.logical_and(z >= 0, z < S)

    barrier = pltpu.get_barrier_semaphore()
    for j in range(1, S):
        pl.semaphore_signal(barrier, inc=1, device_id={"seq": lax.rem(s + j, S)}, device_id_type=MESH)
    for j in range(1, G):
        pl.semaphore_signal(barrier, inc=1, device_id={"groups": lax.rem(g + j, G)}, device_id_type=MESH)
    peers = []
    for j in range(1, TK):
        other = lax.rem(p + j, TK)
        peers.append((j - 1, other, lax.div(other, K), lax.rem(other, K)))
        pl.semaphore_signal(
            barrier, inc=1, device_id={"tp": peers[-1][2], "kv": peers[-1][3]}, device_id_type=MESH
        )

    mine = pl.ds(pl.multiple_of(s * rows, rows), rows)
    stay = pl.ds(pl.multiple_of(s * block, block), block)
    local = [
        pltpu.make_async_copy(a, b, local_sem.at[i])
        for i, (a, b) in enumerate(
            [
                (events.at[s], xb.at[p, stay]),
                (table_in, table),
                (wq_in, wq.at[mine]),
                (history.at[:, 0], hist),
                (wkv_in, wkv.at[:, mine]),
                (wo_in, wo.at[mine]),
                (wc_in, wc.at[:, mine]),
                (dq_in, dq),
                (do_in, do),
            ]
        )
    ]
    for copy in local:
        copy.start()
    pl.semaphore_wait(barrier, (S - 1) + (G - 1) + (TK - 1))

    for j in range(1, S):
        to = lax.rem(s + j, S)
        remote(events.at[to], xb.at[p, stay], ev_send.at[0], ev_recv.at[s], seq=to).start()

    weights = [
        (wq, wq_in, None), (wkv, wkv_in, 0), (wkv, wkv_in, 1),
        (wo, wo_in, None), (wc, wc_in, 0), (wc, wc_in, 1),
    ]
    Q, KEY, VALUE, OUT, CKEY, CVALUE = range(6)
    pieces = [(n, sub, of) for n, of in enumerate(subs_of(S)) for sub in range(of)]
    last = {n: i for i, (n, sub, of) in enumerate(pieces)}

    def view(ref, lead, start, size):
        where = pl.ds(pl.multiple_of(start, size), size)
        return ref.at[where] if lead is None else ref.at[lead, where]

    def at(i, origin):
        n, sub, of = pieces[i]
        size = part // of
        return view(weights[n][0], weights[n][2], origin * rows + g * part + sub * size, size)

    def own(i):
        n, sub, of = pieces[i]
        size = part // of
        return view(weights[n][1], weights[n][2], g * part + sub * size, size)

    up = (2 * s) // S
    ways = (2 * up - 1, 1 - 2 * up)

    def forward(i, way, r):
        step = ways[way]
        origin = s - step * r
        src = own(i) if r == 0 else at(i, origin)
        remote(src, at(i, origin), z_send.at[way, r], z_recv.at[i, origin], seq=s + step).start()

    def begin(i):
        for way in (0, 1):
            pl.when(inside(s + ways[way]))(functools.partial(forward, i, way, 0))

    def arrive(i, way, r):
        step = ways[way]
        origin = s - step * r

        def go():
            piece = at(i, origin)
            wait_recv(piece, z_recv.at[i, origin])
            if r + 1 < S:
                pl.when(inside(s + step))(functools.partial(forward, i, way, r))
            for j in range(1, G):
                remote(
                    piece, piece, y_send.at[way, r - 1, j - 1], y_recv.at[pieces[i][0], origin, j - 1],
                    groups=lax.rem(g + j, G),
                ).start()

        pl.when(inside(origin))(go)

    def settle(n, origin):
        def go():
            for j in range(1, G):
                half_of = view(
                    weights[n][0], weights[n][2], origin * rows + lax.rem(g - j + G, G) * part, part
                )
                wait_recv(half_of, y_recv.at[n, origin, j - 1])

        pl.when(origin != s)(go)

    def settle_all(n):
        for origin in range(S):
            settle(n, origin)

    progress = [0]
    AHEAD = 1
    LAG = 1

    def upto(goal):
        while progress[0] <= min(goal, len(pieces) - 1 + (S - 1) * LAG):
            now = progress[0]
            if now == 0:
                for i in range(min(AHEAD, len(pieces))):
                    begin(i)
            if now + AHEAD < len(pieces):
                begin(now + AHEAD)
            for way in (0, 1):
                for r in reversed(range(1, S)):
                    if 0 <= now - r * LAG < len(pieces):
                        arrive(now - r * LAG, way, r)
            progress[0] += 1

    def arrived(n, r=None):
        upto(last[n] + LAG * (S - 1 if r is None else r))

    unit = part * sum(w[0].shape[-1] for w in weights) // cols

    def finish_weights():
        whole = wq.at[pl.ds(0, unit)]
        for way in (0, 1):
            step = ways[way]
            for r in range(S - 1):
                ok = jnp.logical_and(inside(s + step), inside(s - step * r))
                pl.when(ok)(functools.partial(wait_send, whole, z_send.at[way, r]))
            for r in range(1, S):
                for j in range(1, G):
                    pl.when(inside(s - step * r))(
                        functools.partial(wait_send, whole, y_send.at[way, r - 1, j - 1])
                    )

    def spread(piece_of, send_sem, recv_of):
        def give(source, **where):
            piece = piece_of(source)
            remote(piece, piece, send_sem, recv_of(source), **where).start()

        def take(source):
            wait_recv(piece_of(source), recv_of(source))

        def start():
            for i in range(1, T):
                give(p, tp=lax.rem(t + i, T))
            for j in range(1, K):
                give(p, kv=lax.rem(k + j, K))

        def relay():
            for i in range(1, T):
                there = lax.rem(t - i + T, T) * K + k
                take(there)
                for j in range(1, K):
                    give(there, kv=lax.rem(k + j, K))

        def finish():
            for j in range(1, K):
                for i in range(T):
                    take(lax.rem(t - i + T, T) * K + lax.rem(k - j + K, K))

        return start, relay, finish

    upto(0)

    def came(j):
        return pl.ds(pl.multiple_of(lax.rem(s - j + S, S) * block, block), block)

    moves = [
        spread(lambda q, j=j: xb.at[q, came(j)], xa_send.at[0], lambda q, j=j: xa_recv.at[j, q])
        for j in range(S)
    ]
    local[0].wait()
    moves[0][0]()

    local[1].wait()
    vocab = table.shape[0]
    column = jnp.zeros((steps * beams, 1), jnp.int32)
    line = lax.broadcasted_iota(jnp.int32, column.shape, 0)
    for r in range(steps * beams):
        column = jnp.where(line == r, ids[r // beams, r % beams], column)
    onehot = (
        column == p * vocab + lax.broadcasted_iota(jnp.int32, (steps * beams, vocab), 1)
    ).astype(BF16)
    for kk in range(K):
        for c in range(half // cols if half > cols else 1):
            wide = min(half, cols)
            look_own[kk, :, c * wide : (c + 1) * wide] = dot(
                onehot, table[:, kk * half + c * wide : kk * half + (c + 1) * wide]
            ).astype(BF16)
    for j in range(1, K):
        pk = lax.rem(k + j, K)
        remote(look_own.at[pk], look_in.at[j - 1], lk_send.at[0], lk_recv.at[0, j - 1], kv=pk).start()

    for j in range(1, S):
        wait_recv(xb.at[p, came(j)], ev_recv.at[lax.rem(s - j + S, S)])
        moves[j][0]()
    upto(1)
    moves[0][1]()

    for j in range(1, K):
        wait_recv(look_in.at[j - 1], lk_recv.at[0, j - 1])
    look_sum[...] = (
        look_own[k].astype(F32) + sum(look_in[j].astype(F32) for j in range(K - 1))
    ).astype(BF16)
    for i in range(1, T):
        remote(
            look_sum, look_x.at[i - 1], lk_send.at[1], lk_recv.at[1, i - 1], tp=lax.rem(t + i, T)
        ).start()

    for j in range(1, S):
        moves[j][1]()
    upto(2)
    for j in range(S):
        moves[j][2]()
        lines = came(j)
        source = [xb[q, lines].astype(F32) for q in range(TK)]
        square = sum(jnp.sum(v * v, axis=-1, keepdims=True) for v in source)
        scale = lax.rsqrt(square / width + eps)
        for q in range(TK):
            span = slice(q * cols, (q + 1) * cols)
            normed[lines, span] = (source[q] * scale * egain[:, span]).astype(BF16)
        if j == S // 2:
            upto(3)

    def lines_of(which):
        return pl.ds(pl.multiple_of(which * share, share), share)

    for q in range(TK):
        res[:, q * cols : (q + 1) * cols] = xb[q, lines_of(p)]
    for i in range(1, T):
        wait_recv(look_x.at[i - 1], lk_recv.at[1, i - 1])
    look[k] = (
        look_sum[...].astype(F32) + sum(look_x[i].astype(F32) for i in range(T - 1))
    ).astype(BF16)
    for j in range(1, K):
        remote(look.at[k], look.at[k], lk_send.at[2], lk_recv.at[2, j - 1], kv=lax.rem(k + j, K)).start()
    upto(4)
    for j in range(1, K):
        wait_recv(look.at[lax.rem(k - j + K, K)], lk_recv.at[2, j - 1])

    def code(level):
        lines = slice(level * beams, (level + 1) * beams)
        return jnp.concatenate([look[kk, lines] for kk in range(K)], axis=-1).astype(F32)

    def query(hidden):
        raw = dot((hidden * dgain[...]).astype(BF16), dq[...])
        return (raw * unit_of(hidden)).astype(BF16)

    local[7].wait()
    hidden_ref[...] = code(0)
    queries = query(hidden_ref[...])
    upto(5)

    local[2].wait()
    arrived(Q)
    settle_all(Q)
    qs[...] = dot(normed[...], wq[...]).astype(BF16)

    heads = cols // DH
    ratio = cols // kcols
    limit = counts[0] * BLK
    chunk = min(share, length)
    local[3].wait()
    for h in range(heads):
        hs = slice(h * DH, (h + 1) * DH)
        ks = slice(h // ratio * DH, (h // ratio + 1) * DH)
        for c in range(length // chunk):
            lines = slice(c * chunk, (c + 1) * chunk)
            old[h, lines] = jnp.exp(dot_t(qs[lines, hs], hist[0, :, ks]) * DH ** (-0.5))
        if h == heads // 2 - 1:
            upto(last[Q] + (S - 1) * LAG + 1)
    local[4].wait()
    arrived(KEY)
    settle_all(KEY)
    kn[...] = dot(normed[...], wkv[0]).astype(BF16)
    for h in range(heads):
        hs = slice(h * DH, (h + 1) * DH)
        ks = slice(h // ratio * DH, (h // ratio + 1) * DH)
        for c in range(length // chunk):
            lines = slice(c * chunk, (c + 1) * chunk)
            reach = (c + 1) * chunk
            new = jnp.exp(dot_t(qs[lines, hs], kn[:reach, ks]) * DH ** (-0.5))
            qi = lax.broadcasted_iota(jnp.int32, (chunk, reach), 0) + c * chunk
            ki = lax.broadcasted_iota(jnp.int32, (chunk, reach), 1)
            new = jnp.where((ki <= qi) & (ki < limit), new, 0.0)
            past = old[h, lines]
            total = jnp.sum(past, axis=-1, keepdims=True) + jnp.sum(new, axis=-1, keepdims=True)
            pold[h, lines] = (past / total).astype(BF16)
            pnew[h, lines, :reach] = (new / total).astype(BF16)
        if h == heads // 2 - 1:
            upto(last[KEY] + (S - 1) * LAG + 1)
    arrived(VALUE)
    settle_all(VALUE)
    vn[...] = dot(normed[...], wkv[1]).astype(BF16)
    for h in range(heads):
        hs = slice(h * DH, (h + 1) * DH)
        ks = slice(h // ratio * DH, (h // ratio + 1) * DH)
        for c in range(length // chunk):
            lines = slice(c * chunk, (c + 1) * chunk)
            reach = (c + 1) * chunk
            att[lines, hs] = (
                dot(pold[h, lines], hist[1, :, ks]) + dot(pnew[h, lines, :reach], vn[:reach, ks])
            ).astype(BF16)
    local[5].wait()

    in_turn = chunks == S and S & (S - 1) == 0

    def features(i):
        if not in_turn:
            return i
        at_plane, bit = 0, 1
        while bit < S:
            here = lax.rem(lax.div(s, bit), 2)
            at_plane = at_plane + bit * (1 - here if i & bit else here)
            bit *= 2
        return at_plane

    def span_of(i):
        return pl.ds(pl.multiple_of(features(i) * feats, feats), feats)

    def project(i):
        gterm[i] = dot_t(att[...], wo[span_of(i), :]).astype(BF16)
        for j in range(1, K):
            pk = lax.rem(k + j, K)
            for it in range(T):
                remote(
                    gterm.at[i, lines_of(lax.rem(t + 1 + it, T) * K + pk)], rk.at[i, j - 1, it],
                    rk_send.at[0], rk_recv.at[i, j - 1], kv=pk,
                ).start()

    def pass_on(i):
        for j in range(1, K):
            wait_recv(rk.at[i, j - 1], rk_recv.at[i, j - 1])
        for it in range(T):
            to = lax.rem(t + 1 + it, T)
            total = gterm[i, lines_of(to * K + k)].astype(F32)
            for j in range(1, K):
                total = total + rk[i, j - 1, it].astype(F32)
            if it < T - 1:
                s1[i, it] = total.astype(BF16)
                remote(s1.at[i, it], rt.at[i, it], rt_send.at[0], rt_recv.at[i, it], tp=to).start()
            else:
                acc[i] = total

    gathers = [
        spread(
            lambda q, i=i: cx.at[features(i), lines_of(q)], cg_send.at[0], lambda q, i=i: cg_recv.at[i, q]
        )
        for i in range(chunks)
    ]
    squares = []

    def complete(i):
        value = acc[i]
        for it in range(T - 1):
            wait_recv(rt.at[i, it], rt_recv.at[i, it])
            value = value + rt[i, it].astype(F32)
        value = value + res[:, span_of(i)].astype(F32)
        squares.append(jnp.sum(value * value, axis=-1, keepdims=True))
        cx[features(i), lines_of(p)] = (value * cgain[:, span_of(i)]).astype(BF16)
        gathers[i][0]()
        enc_out[:, span_of(i)] = value.astype(BF16)

    if not in_turn:
        arrived(OUT)
        settle_all(OUT)
    for i in range(chunks + 5):
        if i < chunks:
            if in_turn:
                arrived(OUT, i)
                if i > 0:
                    settle(OUT, features(i))
            project(i)
        else:
            upto(last[OUT] + (S - 1) * LAG + 1 + i - chunks)
        if 1 <= i < chunks + 1:
            pass_on(i - 1)
        if 2 <= i < chunks + 2:
            complete(i - 2)
            if i == chunks + 2 - 1:
                scale = lax.rsqrt(sum(squares) / width + eps)
                sc[p] = jnp.broadcast_to(scale, (share, 128))
                for slot, other, pt, pk in peers:
                    remote(sc.at[p], sc.at[p], sc_send.at[0], sc_recv.at[p], tp=pt, kv=pk).start()
        if 4 <= i < chunks + 4:
            gathers[i - 4][1]()
    arrived(CKEY)
    for slot, other, pt, pk in peers:
        wait_recv(sc.at[other], sc_recv.at[other])
    for start, relay, finish in gathers:
        finish()
    local[6].wait()
    settle_all(CKEY)
    by_row = sc[...].reshape(length, 128)[:, :1]

    def across(which):
        total = dot(cx[0], wc[which, :feats])
        for c in range(1, chunks):
            total = total + dot(cx[c], wc[which, c * feats : (c + 1) * feats])
        return (total * by_row).astype(BF16)

    ck[...] = across(0)
    live = lax.broadcasted_iota(jnp.int32, (ratio * beams, length), 1) < limit

    def soften(queries, j):
        ks = slice(j * DH, (j + 1) * DH)
        q = jnp.concatenate(
            [queries[:, (j * ratio + a) * DH : (j * ratio + a + 1) * DH] for a in range(ratio)], axis=0
        )
        raised = jnp.where(live, jnp.exp(dot_t(q, ck[:, ks]) * DH ** (-0.5)), 0.0)
        return (raised / jnp.sum(raised, axis=-1, keepdims=True)).astype(BF16)

    soft = [soften(queries, j) for j in range(kcols // DH)]
    local[8].wait()
    arrived(CVALUE)
    settle_all(CVALUE)
    cv[...] = across(1)

    for level in range(steps):
        if level > 0:
            soft = [soften(queries, j) for j in range(kcols // DH)]
        for j in range(kcols // DH):
            ks = slice(j * DH, (j + 1) * DH)
            found = dot(soft[j], cv[:, ks]).astype(BF16)
            for a in range(ratio):
                h = j * ratio + a
                ba[:, h * DH : (h + 1) * DH] = found[a * beams : (a + 1) * beams]
        if level < steps - 1:
            column = jnp.zeros((beams, 1), jnp.int32)
            line = lax.broadcasted_iota(jnp.int32, column.shape, 0)
            for r in range(beams):
                column = jnp.where(line == r, parents[level, r], column)
            pick = column == lax.broadcasted_iota(jnp.int32, (beams, beams), 1)
            picked = dot(pick.astype(BF16), ba[...]).astype(BF16)
            for c in range(TK):
                terms[level, p, c] = dot_t(picked, do[c * cols : (c + 1) * cols, :]).astype(BF16)
            for slot, other, pt, pk in reversed(peers):
                piece = terms.at[level, p]
                remote(piece, piece, tm_send.at[0], tm_recv.at[level, p], tp=pt, kv=pk).start()
            moved = jnp.dot(
                pick.astype(F32), hidden_ref[...], preferred_element_type=F32, precision=lax.Precision.HIGHEST
            )
            hidden_ref[...] = moved + code(level + 1)
            for slot, other, pt, pk in peers:
                wait_recv(terms.at[level, other], tm_recv.at[level, other])
            for c in range(TK):
                span = slice(c * cols, (c + 1) * cols)
                hidden_ref[:, span] = hidden_ref[:, span] + sum(
                    terms[level, q, c].astype(F32) for q in range(TK)
                )
            queries = query(hidden_ref[...])
        else:
            for c in range(TK):
                last_own[c] = dot_t(ba[...], do[c * cols : (c + 1) * cols, :]).astype(BF16)
            for slot, other, pt, pk in peers:
                remote(
                    last_own.at[other], last_in.at[slot], tm_send.at[1], tm_recv.at[level, slot], tp=pt, kv=pk
                ).start()
            value = jnp.zeros((beams, cols), F32)
            for c in range(TK):
                span = slice(c * cols, (c + 1) * cols)
                value = jnp.where(p == c, hidden_ref[:, span], value)
            value = value + last_own[p].astype(F32)
            for slot, other, pt, pk in peers:
                wait_recv(last_in.at[slot], tm_recv.at[level, slot])
            for slot in range(TK - 1):
                value = value + last_in[slot].astype(F32)
            beam_out[...] = value.astype(BF16)

    finish_weights()
    wait_send(xb.at[0, pl.ds(0, (S - 1) * block)], ev_send.at[0])
    wait_send(xb.at[pl.ds(0, TK - 1)], xa_send.at[0])
    wait_send(look_in, lk_send.at[0])
    wait_send(look_x, lk_send.at[1])
    wait_send(look_in, lk_send.at[2])
    wait_send(rk, rk_send.at[0])
    wait_send(rt, rt_send.at[0])
    wait_send(cx.at[:, pl.ds(0, (TK - 1) * share)], cg_send.at[0])
    wait_send(sc.at[pl.ds(0, TK - 1)], sc_send.at[0])
    wait_send(terms.at[pl.ds(0, steps - 1), pl.ds(0, TK - 1)], tm_send.at[0])
    wait_send(last_in, tm_send.at[1])


def solution(mesh):
    G, S, T, K = (mesh.shape[a] for a in ("groups", "seq", "tp", "kv"))
    TK = T * K

    def shards(
        events, history, counts, ids, parents, wq, wkv, wo, wc, dq, do, table, egain, cgain, dgain
    ):
        users, block, cols = events.shape
        length = block * S
        share = length // TK
        rows, kcols = wkv.shape[1:]
        width = rows * S
        steps, beams = ids.shape
        hist_len = history.shape[2]
        heads = cols // DH
        chunks = S if rows % 128 == 0 else TK
        feats = width // chunks
        pieces = sum(subs_of(S))
        vm = lambda *shape: pltpu.VMEM(shape, BF16)
        vf = lambda *shape: pltpu.VMEM(shape, F32)
        dma = lambda *shape: pltpu.SemaphoreType.DMA(shape)
        anywhere = pl.BlockSpec(memory_space=pl.ANY)
        vmem = pl.BlockSpec(memory_space=pltpu.VMEM)
        smem = pl.BlockSpec(memory_space=pltpu.SMEM)
        enc, beam = pl.pallas_call(
            functools.partial(body, (G, S, T, K)),
            out_shape=(
                jax.ShapeDtypeStruct((share, width), BF16),
                jax.ShapeDtypeStruct((beams, cols), BF16),
            ),
            in_specs=[anywhere, anywhere, smem, smem, smem] + [anywhere] * 7 + [vmem] * 3,
            out_specs=(vmem, vmem),
            scratch_shapes=[
                vm(width, cols), vm(2, width, kcols), vm(width, cols), vm(2, width, kcols),
                vm(width, cols), vm(width, cols), vm(*table.shape), vm(2, hist_len, kcols),
                vm(TK, length, cols), vm(length, width), vm(share, width),
                vm(length, cols), vm(length, kcols), vm(length, kcols),
                vf(heads, length, hist_len), vm(heads, length, hist_len), vm(heads, length, length),
                vm(length, cols),
                vm(chunks, length, feats), vm(chunks, K - 1, T, share, feats),
                vm(chunks, T - 1, share, feats), vm(chunks, T - 1, share, feats),
                vf(chunks, share, feats), vm(chunks, length, feats), vf(TK, share, 128),
                vm(length, kcols), vm(length, kcols),
                vm(K, steps * beams, width // K), vm(K - 1, steps * beams, width // K),
                vm(steps * beams, width // K), vm(T - 1, steps * beams, width // K),
                vm(K, steps * beams, width // K),
                vm(steps - 1, TK, TK, beams, cols), vm(TK, beams, cols), vm(TK - 1, beams, cols),
                vf(beams, width), vm(beams, cols),
                dma(9), dma(2, S - 1), dma(pieces, S), dma(2, S - 1, G - 1), dma(6, S, G - 1),
                dma(1), dma(S), dma(1), dma(S, TK),
                dma(3), dma(3, max(T, K) - 1), dma(1), dma(chunks, K - 1), dma(1), dma(chunks, T - 1),
                dma(1), dma(chunks, TK), dma(1), dma(TK),
                dma(2), dma(steps, TK),
            ],
            compiler_params=pltpu.CompilerParams(
                collective_id=0, has_side_effects=True, vmem_limit_bytes=60 * 1024 * 1024
            ),
        )(
            events, history, counts, ids, parents, wq, wkv, wo, wc, dq, do,
            table, egain[None], cgain[None], dgain[None],
        )
        return enc[None], beam

    in_specs = (
        P("groups", "seq", ("tp", "kv")),
        P(None, ("groups", "seq"), None, ("tp", "kv")),
        P(("groups", "seq")),
        P(None, ("groups", "seq")),
        P(None, ("groups", "seq")),
        P("seq", ("tp", "kv")),
        P(None, "seq", ("tp", "kv")),
        P("seq", ("tp", "kv")),
        P(None, "seq", ("tp", "kv")),
        P(None, ("tp", "kv")),
        P(None, ("tp", "kv")),
        P(("tp", "kv"), None),
        P(),
        P(),
        P(),
    )
    out_specs = (P(("groups", "seq"), ("tp", "kv"), None), P(("groups", "seq"), ("tp", "kv")))
    return jax.shard_map(shards, mesh=mesh, in_specs=in_specs, out_specs=out_specs, check_vma=False)
```
